32 devices in a mesh: ctx: 8 (over z, y), grp: 4 (over x, core).
Axes of the slice: x: 2, y: 2, z: 4, core: 2. Of those that a mesh axis runs over, the one named last changes fastest.
Arguments:
- streams: bfloat16 [3, 3072, 4096], P(None, 'ctx', 'grp'), may hold values from -400 to 400
- filters: bfloat16 [3, 256, 128], P(None, 'grp'), may hold values from -0.5 to 0.5
- gain: float32 [4096], P('grp'), may hold values from 0.5 to 1.5
Outputs:
- normed: bfloat16 [3072, 4096], P('ctx', 'grp')
The draws below stay inside these ranges and needn't reach their ends.
All inputs are finite; a program needn't handle non-finite values.
Results may differ from the reference program's by a relative error of at most 0.012.
The reference program's roundings to bfloat16 on the way count: a program that leaves them out, or rounds other values in their place, can miss the bound.
Values may be sent and summed in bfloat16 or wider, within the bound.
A program may use at most 128 MiB of HBM per device.

```python
import math
import jax
import jax.numpy as jnp
import numpy as np
from jax import lax

HEADS = 32
HD = 128
FG = 256
FLEN = 128
CH = 4096
LEN = 3072


def draw_streams(key, part):
    key_list = jax.random.split(key, 2)
    base = jnp.clip(jax.random.normal(key_list[0], (3, LEN, CH), jnp.float32), -4.0, 4.0)
    chan_top = 10.0
    chan_scale = jnp.exp(math.log(chan_top) * jnp.arange(CH, dtype=jnp.float32) / (CH - 1))
    tok_scale = jnp.exp(jax.random.uniform(key_list[1], (LEN,), jnp.float32, 0.0, math.log(3.0)))
    base = base.at[2].multiply(tok_scale[:, None] * chan_scale[None, :])
    return base.astype(jnp.bfloat16)


def level_of(own_key, extent, shards, least, largest):
    factor_of = 1.0
    for dim, shards_of in shards:
        draws = jax.random.uniform(jax.random.fold_in(jax.random.fold_in(own_key, 6), dim), (shards_of,), jnp.float32, least / len(shards), largest / len(shards))
        factor_of = factor_of * jnp.repeat(jnp.exp(draws), extent[dim] // shards_of).reshape((-1,) + (1,) * (len(extent) - 1 - dim))
    return factor_of


def scatter_about(stream_key, extent, width, most, shards=(), kind=jnp.bfloat16):
    level = level_of(stream_key, extent, shards, -0.22, 0.18) if shards else 1.0
    values = jax.random.normal(stream_key, extent, jnp.float32) * width * level
    return jnp.minimum(jnp.maximum(values, -most), most).astype(kind)


def setup_inputs(seed: int = 0) -> dict:
    key_of = jax.random.split(jax.random.key(seed), 4)
    return {
        "streams": draw_streams(jax.random.fold_in(key_of[3], 71), 0),
        "filters": scatter_about(key_of[1], (3, FG, FLEN), FLEN ** -0.5, 0.5, ((1, 4),)),
        "gain": jnp.clip(1.0 + 0.1 * jax.random.normal(key_of[2], (CH,), jnp.float32), 0.5, 1.5),
    }


def filter_stream(values, taps):
    group_width = CH // FG
    block_count = LEN // FLEN
    lag_table = np.arange(FLEN)[:, None] - np.arange(FLEN)[None, :]
    lower_idx = np.where(lag_table >= 0, lag_table, 0)
    upper_idx = np.where(lag_table < 0, lag_table + FLEN, 0)
    taps_wide = taps.astype(jnp.float32)
    lower = jnp.where(lag_table >= 0, taps_wide[:, lower_idx], 0.0)
    upper = jnp.where(lag_table < 0, taps_wide[:, upper_idx], 0.0)
    wide = values.astype(jnp.float32)
    padded = jnp.concatenate([jnp.zeros((FLEN, CH), wide.dtype), wide], axis=0)
    blocks = padded.reshape(block_count + 1, FLEN, FG, group_width)
    result = jnp.einsum('gts,bsgc->btgc', lower, blocks[1:], precision=lax.Precision.HIGHEST)
    result = result + jnp.einsum('gts,bsgc->btgc', upper, blocks[:-1], precision=lax.Precision.HIGHEST)
    return result.reshape(LEN, CH).astype(jnp.bfloat16)

def reference(streams, filters, gain):
    features = [filter_stream(streams[idx], filters[idx]) for idx in range(3)]
    split = [feat.reshape(LEN, HEADS, HD).transpose(1, 0, 2) for feat in features]
    block_rows = math.gcd(LEN, 1024)
    outputs = []
    for block_idx in range(LEN // block_rows):
        first = block_idx * block_rows
        key_len = first + block_rows
        query_pos = first + jnp.arange(block_rows, dtype=jnp.int32)
        key_pos = jnp.arange(key_len, dtype=jnp.int32)
        causal = query_pos[:, None] >= key_pos[None, :]

        def head_attention(triple):
            query, keyed, valued = triple
            scores = jnp.dot(query, keyed.T, preferred_element_type=jnp.float32) * HD ** (-0.5)
            top = lax.optimization_barrier(jnp.max(jnp.where(causal, scores, -1e+30), axis=1))
            weights = jnp.where(causal, jnp.exp(scores - top[:, None]), 0.0)
            numer = jnp.dot(weights.astype(jnp.bfloat16), valued, preferred_element_type=jnp.float32)
            return (numer / lax.optimization_barrier(jnp.sum(weights, axis=1))[:, None]).astype(jnp.bfloat16)
        per_head = lax.map(head_attention, (split[0][:, first:key_len], split[1][:, :key_len], split[2][:, :key_len]))
        outputs.append(per_head.transpose(1, 0, 2).reshape(block_rows, CH))
    attended = jnp.concatenate(outputs, axis=0)
    wide = attended.astype(jnp.float32)
    power = lax.optimization_barrier(jnp.mean(wide * wide, axis=1))
    return (wide * gain[None, :] / jnp.sqrt(power + 1e-06)[:, None]).astype(jnp.bfloat16)
```

```python
import functools
import math

import jax
import jax.numpy as jnp
import numpy as np
from jax import lax
from jax.experimental import pallas as pl
from jax.experimental.pallas import tpu as pltpu
from jax.sharding import PartitionSpec as P

HD = 128
LANES = 128
MESH = pl.DeviceIdType.MESH


def fused_kernel(
    n,
    n_grp,
    streams,
    filters,
    gain,
    out,
    buf,
    taps,
    toep,
    feat,
    scores,
    top,
    total,
    accum,
    sending,
    att,
    sums,
    local_sem,
    send_sem,
    recv_sem,
    back_send,
    back_recv,
    sum_send,
    sum_recv,
):
    me = lax.axis_index("ctx")
    my_grp = lax.axis_index("grp")
    rows = streams.shape[1]
    chans = streams.shape[2]
    groups = filters.shape[1]
    flen = filters.shape[2]
    cols = chans // n
    width = chans // groups
    own_groups = groups // n
    per_tile = LANES // width
    heads = cols // HD

    def col_of(j):
        return pl.ds(pl.multiple_of(j * cols, cols), cols)

    def row_of(i):
        return pl.ds(pl.multiple_of(flen + i * rows, flen), rows)

    barrier = pltpu.get_barrier_semaphore()
    for k in range(1, n):
        pl.semaphore_signal(
            barrier, inc=1, device_id={"ctx": lax.rem(me + k, n)}, device_id_type=MESH
        )
    for k in range(1, n_grp):
        pl.semaphore_signal(
            barrier, inc=1, device_id={"grp": lax.rem(my_grp + k, n_grp)}, device_id_type=MESH
        )
    pl.semaphore_wait(barrier, n - 1 + n_grp - 1)

    def stream_copy(s, target, source):
        return pltpu.make_async_remote_copy(
            src_ref=streams.at[s, :, col_of(target)],
            dst_ref=buf.at[s, row_of(source), :],
            send_sem=send_sem.at[target, s],
            recv_sem=recv_sem.at[source, s],
            device_id={"ctx": target},
            device_id_type=MESH,
        )

    def own_copy(s):
        return pltpu.make_async_copy(
            streams.at[s, :, col_of(me)], buf.at[s, row_of(me), :], local_sem.at[s]
        )

    for k in range(1, n):
        target = lax.rem(me + k, n)
        for s in range(3):
            stream_copy(s, target, me).start()
    for s in range(3):
        own_copy(s).start()

    for s in range(3):
        buf[s, pl.ds(0, flen), :] = jnp.zeros((flen, cols), buf.dtype)
    taps[...] = filters[...].astype(jnp.float32)
    row_id = lax.broadcasted_iota(jnp.int32, (flen, flen), 0)
    col_id = lax.broadcasted_iota(jnp.int32, (flen, flen), 1)

    @pl.loop(0, 3 * own_groups)
    def _(idx):
        s = idx // own_groups
        g = lax.rem(idx, own_groups)
        line = taps[s, pl.ds(me * own_groups + g, 1), :]
        turned = pltpu.roll(
            jnp.broadcast_to(line, (flen, flen)), 0, 1, stride=1, stride_axis=0
        ).T
        lower = jnp.where(col_id <= row_id, turned, 0.0)
        upper = jnp.where(col_id > row_id, turned, 0.0)
        where = pl.ds(pl.multiple_of(g * flen, flen), flen)
        toep[s, where, pl.ds(0, flen)] = upper.astype(toep.dtype)
        toep[s, where, pl.ds(flen, flen)] = lower.astype(toep.dtype)

    blocks = rows // flen
    lane_group = lax.broadcasted_iota(jnp.int32, (flen, blocks * LANES), 1)
    lane_group = lax.rem(lane_group, LANES) // width
    factor = HD ** (-0.5) * math.log2(math.e)

    def fold(values, op):
        result = values[:, :LANES]
        for c in range(1, values.shape[1] // LANES):
            result = op(result, values[:, c * LANES : (c + 1) * LANES])
        return result

    def filter_block(i):
        @pl.loop(0, 3)
        def _(s):
            for h in range(heads):
                lanes = pl.ds(h * LANES, LANES)
                window = [
                    buf[s, pl.ds(pl.multiple_of(i * rows + b * flen, flen), 2 * flen), lanes]
                    for b in range(blocks)
                ]
                matrix = toep[s, pl.ds(h * per_tile * flen, per_tile * flen), :]
                product = jnp.dot(
                    matrix, jnp.concatenate(window, axis=1), preferred_element_type=jnp.float32
                )
                result = product[:flen]
                for g in range(1, per_tile):
                    result = jnp.where(
                        lane_group == g, product[g * flen : (g + 1) * flen], result
                    )
                result = result.astype(feat.dtype)
                for b in range(blocks):
                    feat[
                        s, pl.ds(pl.multiple_of(i * rows + b * flen, flen), flen), lanes
                    ] = result[:, b * LANES : (b + 1) * LANES]

    def rows_at(j):
        return pl.ds(pl.multiple_of(j * rows, flen), rows)

    def attend_block(i, h):
        lanes = pl.ds(h * HD, HD)
        query = feat[0, rows_at(i), lanes]

        def score(j):
            return lax.dot_general(
                query,
                feat[1, rows_at(j), lanes],
                (((1,), (1,)), ((), ())),
                preferred_element_type=jnp.float32,
            )

        place = lax.broadcasted_iota(jnp.int32, (rows, rows), 0)
        other = lax.broadcasted_iota(jnp.int32, (rows, rows), 1)
        diagonal = jnp.where(other <= place, score(i), -1e30)
        scores[i] = diagonal
        top[...] = fold(diagonal, jnp.maximum)

        @pl.loop(0, i)
        def _(j):
            block = score(j)
            scores[j] = block
            top[...] = jnp.maximum(top[...], fold(block, jnp.maximum))

        highest = jnp.max(top[...], axis=1, keepdims=True)
        top[...] = jnp.broadcast_to(highest, top.shape)
        total[...] = jnp.zeros_like(total)
        accum[...] = jnp.zeros_like(accum)

        @pl.loop(0, i + 1)
        def _(j):
            weights = jnp.exp2((scores[j] - top[:, :1]) * factor)
            total[...] += fold(weights, jnp.add)
            accum[...] += jnp.dot(
                weights.astype(jnp.bfloat16),
                feat[2, rows_at(j), lanes],
                preferred_element_type=jnp.float32,
            )

        sum_of = jnp.sum(total[...], axis=1, keepdims=True)
        return (accum[...] / sum_of).astype(jnp.bfloat16)

    def back_copy(target, source):
        return pltpu.make_async_remote_copy(
            src_ref=sending.at[target],
            dst_ref=att.at[:, col_of(source)],
            send_sem=back_send.at[target],
            recv_sem=back_recv.at[source],
            device_id={"ctx": target},
            device_id_type=MESH,
        )

    @pl.loop(0, n)
    def _(i):
        @pl.when(i != me)
        def _():
            for s in range(3):
                stream_copy(s, i, i).wait_recv()

        @pl.when(i == me)
        def _():
            for s in range(3):
                own_copy(s).wait()

        filter_block(i)
        for h in range(heads):
            sending[i, :, pl.ds(h * HD, HD)] = attend_block(i, h)

        @pl.when(i != me)
        def _():
            back_copy(i, me).start()

        @pl.when(i == me)
        def _():
            att[:, col_of(me)] = sending[i]

    for k in range(1, n):
        source = lax.rem(me + k, n)
        back_copy(source, source).wait_recv()

    @pl.loop(0, blocks)
    def _(b):
        part = pl.ds(pl.multiple_of(b * flen, flen), flen)
        wide = att[part, :].astype(jnp.float32)
        squares = fold(wide * wide, jnp.add).T
        squares = squares.reshape(LANES // 8, 8, flen)
        sums[0, :, part] = jnp.sum(squares, axis=0)

    def sum_copy(k, turn):
        return pltpu.make_async_remote_copy(
            src_ref=sums.at[0],
            dst_ref=sums.at[k],
            send_sem=sum_send.at[k],
            recv_sem=sum_recv.at[k],
            device_id={"grp": lax.rem(my_grp + turn, n_grp)},
            device_id_type=MESH,
        )

    for k in range(1, n_grp):
        sum_copy(k, k).start()
    for k in range(1, n_grp):
        sum_copy(k, k).wait()

    @pl.loop(0, blocks)
    def _(b):
        part = pl.ds(pl.multiple_of(b * flen, flen), flen)
        power = sums[0, :, part]
        for k in range(1, n_grp):
            power = power + sums[k, :, part]
        power = jnp.sum(power, axis=0, keepdims=True) / (chans * n_grp)
        power = jnp.broadcast_to(lax.rsqrt(power + 1e-06), (LANES, flen)).T
        wide = att[part, :].astype(jnp.float32)
        for c in range(chans // LANES):
            lanes = slice(c * LANES, (c + 1) * LANES)
            out[part, lanes] = (wide[:, lanes] * gain[:, lanes] * power).astype(out.dtype)

    for k in range(1, n):
        target = lax.rem(me + k, n)
        for s in range(3):
            stream_copy(s, target, me).wait_send()
        back_copy(target, me).wait_send()


def fused(streams, filters, gain):
    n, n_grp = lax.axis_size("ctx"), lax.axis_size("grp")
    _, rows, chans = streams.shape
    _, groups, flen = filters.shape
    cols = chans // n
    tokens = rows * n
    vmem = pl.BlockSpec(memory_space=pltpu.VMEM)
    return pl.pallas_call(
        functools.partial(fused_kernel, n, n_grp),
        out_shape=jax.ShapeDtypeStruct((rows, chans), jnp.bfloat16),
        in_specs=[pl.BlockSpec(memory_space=pl.ANY), vmem, vmem],
        out_specs=vmem,
        scratch_shapes=[
            pltpu.VMEM((3, flen + tokens, cols), jnp.bfloat16),
            pltpu.VMEM((3, groups, flen), jnp.float32),
            pltpu.VMEM((3, groups // n * flen, 2 * flen), jnp.bfloat16),
            pltpu.VMEM((3, tokens, cols), jnp.bfloat16),
            pltpu.VMEM((n, rows, rows), jnp.float32),
            pltpu.VMEM((rows, LANES), jnp.float32),
            pltpu.VMEM((rows, LANES), jnp.float32),
            pltpu.VMEM((rows, HD), jnp.float32),
            pltpu.VMEM((n, rows, cols), jnp.bfloat16),
            pltpu.VMEM((rows, chans), jnp.bfloat16),
            pltpu.VMEM((n_grp, 8, rows), jnp.float32),
            pltpu.SemaphoreType.DMA((3,)),
            pltpu.SemaphoreType.DMA((n, 3)),
            pltpu.SemaphoreType.DMA((n, 3)),
            pltpu.SemaphoreType.DMA((n,)),
            pltpu.SemaphoreType.DMA((n,)),
            pltpu.SemaphoreType.DMA((n_grp,)),
            pltpu.SemaphoreType.DMA((n_grp,)),
        ],
        compiler_params=pltpu.CompilerParams(collective_id=0, has_side_effects=True),
        name="fused",
    )(streams, filters, gain.reshape(1, chans))


def passed_along(block, axis, distance):
    devices = range(lax.axis_size(axis))
    route = [(i - distance, i) for i in devices if i - distance in devices]
    return lax.ppermute(block, axis, route)


def filter_all(streams, filters):
    tok_rows = streams.shape[1]
    chan_count = streams.shape[2]
    filt_len = filters.shape[2]
    group_count = filters.shape[1]
    group_width = chan_count // group_count
    tail = streams[:, tok_rows - filt_len :, :]
    before = passed_along(tail, "ctx", 1)
    padded = jnp.concatenate([before, streams], axis=1)
    block_count = tok_rows // filt_len
    blocks = padded.reshape(3, block_count + 1, filt_len, group_count, group_width)
    lag_table = np.arange(filt_len)[:, None] - np.arange(filt_len)[None, :]
    lower_idx = np.where(lag_table >= 0, lag_table, 0)
    upper_idx = np.where(lag_table < 0, lag_table + filt_len, 0)
    lower = jnp.where(lag_table >= 0, filters[:, :, lower_idx], 0.0)
    upper = jnp.where(lag_table < 0, filters[:, :, upper_idx], 0.0)
    result = jnp.einsum(
        "agts,absgc->abtgc", lower, blocks[:, 1:], preferred_element_type=jnp.float32
    )
    result = result + jnp.einsum(
        "agts,absgc->abtgc", upper, blocks[:, :-1], preferred_element_type=jnp.float32
    )
    return result.reshape(3, tok_rows, chan_count).astype(jnp.bfloat16)


def attend(queries, positions, keyed, valued):
    tok_rows, chan_count = queries.shape
    head_count = chan_count // HD
    scale = HD ** (-0.5)
    query_heads = queries.reshape(tok_rows, head_count, HD)
    query_last = jnp.max(positions)
    start_state = (
        jnp.full((head_count, tok_rows), -1e30, jnp.float32),
        jnp.zeros((head_count, tok_rows), jnp.float32),
        jnp.zeros((tok_rows, head_count, HD), jnp.float32),
    )
    key_piece = lax.all_gather(keyed, "ctx", axis=0, tiled=True)
    value_piece = lax.all_gather(valued, "ctx", axis=0, tiled=True)
    piece_len = key_piece.shape[0]
    block_len = math.gcd(piece_len, 512)

    def step_block(step_idx, state):
        offset = step_idx * block_len
        key_block = lax.dynamic_slice_in_dim(key_piece, offset, block_len, 0).reshape(
            block_len, head_count, HD
        )
        value_block = lax.dynamic_slice_in_dim(value_piece, offset, block_len, 0).reshape(
            block_len, head_count, HD
        )
        key_pos = offset + jnp.arange(block_len, dtype=jnp.int32)

        def update_block(inner):
            running, totals, accum = inner
            scores = (
                jnp.einsum(
                    "shd,khd->hsk", query_heads, key_block, preferred_element_type=jnp.float32
                )
                * scale
            )
            causal = key_pos[None, None, :] <= positions[None, :, None]
            newtop = jnp.maximum(running, jnp.max(jnp.where(causal, scores, -1e30), axis=2))
            weights = jnp.where(causal, jnp.exp(scores - newtop[:, :, None]), 0.0)
            factor = jnp.exp(running - newtop)
            totals = totals * factor + jnp.sum(weights, axis=2)
            accum = accum * factor.T[:, :, None] + jnp.einsum(
                "hsk,khd->shd",
                weights.astype(jnp.bfloat16),
                value_block,
                preferred_element_type=jnp.float32,
            )
            return (newtop, totals, accum)

        return lax.cond(offset > query_last, lambda inner: inner, update_block, state)

    running, totals, accum = lax.fori_loop(0, piece_len // block_len, step_block, start_state)
    return (accum / totals.T[:, :, None]).reshape(tok_rows, chan_count).astype(jnp.bfloat16)


def local(streams, filters, gain):
    features = filter_all(streams, filters)
    tok_rows = streams.shape[1]
    my_index = lax.axis_index("ctx")
    queries = features[0]
    positions = my_index * tok_rows + jnp.arange(tok_rows, dtype=jnp.int32)
    attended = attend(queries, positions, features[1], features[2])
    wide = attended.astype(jnp.float32)
    power = lax.psum(jnp.sum(wide * wide, axis=1), "grp") / (streams.shape[2] * lax.axis_size("grp"))
    return (wide * gain[None, :] * lax.rsqrt(power + 1e-06)[:, None]).astype(jnp.bfloat16)


def chosen(streams, filters, gain):
    n = lax.axis_size("ctx")
    _, rows, chans = streams.shape
    _, groups, flen = filters.shape
    whole_heads = chans % (n * HD) == 0
    fits = flen == LANES and rows % flen == 0 and LANES % (chans // groups) == 0
    if n > 1 and whole_heads and fits and groups % n == 0:
        return fused(streams, filters, gain)
    return local(streams, filters, gain)


def solution(mesh):
    placed = (P(None, "ctx", "grp"), P(None, "grp", None), P("grp"))
    return jax.shard_map(
        chosen, mesh=mesh, in_specs=placed, out_specs=P("ctx", "grp"), check_vma=False
    )
```

```python
import functools
import math

import jax
import jax.numpy as jnp
import numpy as np
from jax import lax
from jax.experimental import pallas as pl
from jax.experimental.pallas import tpu as pltpu
from jax.sharding import PartitionSpec as P

HD = 128
LANES = 128
MESH = pl.DeviceIdType.MESH


def fused_kernel(
    n,
    n_grp,
    streams,
    filters,
    gain,
    out,
    buf,
    taps,
    toep,
    feat,
    top,
    total,
    accum,
    sending,
    att,
    sums,
    local_sem,
    send_sem,
    recv_sem,
    back_send,
    back_recv,
    sum_send,
    sum_recv,
):
    me = lax.axis_index("ctx")
    my_grp = lax.axis_index("grp")
    rows = streams.shape[1]
    chans = streams.shape[2]
    groups = filters.shape[1]
    flen = filters.shape[2]
    cols = chans // n
    width = chans // groups
    own_groups = groups // n
    per_tile = LANES // width
    heads = cols // HD

    def col_of(j):
        return pl.ds(pl.multiple_of(j * cols, cols), cols)

    def row_of(i):
        return pl.ds(pl.multiple_of(flen + i * rows, flen), rows)

    barrier = pltpu.get_barrier_semaphore()
    for k in range(1, n):
        pl.semaphore_signal(
            barrier, inc=1, device_id={"ctx": lax.rem(me + k, n)}, device_id_type=MESH
        )
    for k in range(1, n_grp):
        pl.semaphore_signal(
            barrier, inc=1, device_id={"grp": lax.rem(my_grp + k, n_grp)}, device_id_type=MESH
        )
    pl.semaphore_wait(barrier, n - 1 + n_grp - 1)

    def target_at(k):
        return jnp.bitwise_xor(me, k) if n & (n - 1) == 0 else lax.rem(me + k, n)

    def source_at(k):
        return jnp.bitwise_xor(me, k) if n & (n - 1) == 0 else lax.rem(me - k + n, n)

    spans = ((rows - flen, flen), (0, rows - flen))

    def stream_copy(p, target, source):
        first, size = spans[p]
        start = pl.multiple_of(flen + source * rows + first, flen)
        return pltpu.make_async_remote_copy(
            src_ref=streams.at[:, pl.ds(first, size), col_of(target)],
            dst_ref=buf.at[:, pl.ds(start, size), :],
            send_sem=send_sem.at[target, p],
            recv_sem=recv_sem.at[source, p],
            device_id={"ctx": target},
            device_id_type=MESH,
        )

    def own_copy():
        return pltpu.make_async_copy(
            streams.at[:, :, col_of(me)], buf.at[:, row_of(me), :], local_sem.at[0]
        )

    own_copy().start()
    for p in range(2):
        for k in range(1, n):
            stream_copy(p, target_at(k), me).start()

    for s in range(3):
        buf[s, pl.ds(0, flen), :] = jnp.zeros((flen, cols), buf.dtype)
    taps[...] = filters[...].astype(jnp.float32)
    row_id = lax.broadcasted_iota(jnp.int32, (flen, flen), 0)
    col_id = lax.broadcasted_iota(jnp.int32, (flen, flen), 1)

    @pl.loop(0, 3 * own_groups)
    def _(idx):
        s = idx // own_groups
        g = lax.rem(idx, own_groups)
        line = taps[s, pl.ds(me * own_groups + g, 1), :]
        turned = pltpu.roll(
            jnp.broadcast_to(line, (flen, flen)), 0, 1, stride=1, stride_axis=0
        ).T
        lower = jnp.where(col_id <= row_id, turned, 0.0)
        upper = jnp.where(col_id > row_id, turned, 0.0)
        where = pl.ds(pl.multiple_of(g * flen, flen), flen)
        toep[s, where, pl.ds(0, flen)] = upper.astype(toep.dtype)
        toep[s, where, pl.ds(flen, flen)] = lower.astype(toep.dtype)

    blocks = rows // flen
    lane_group = lax.broadcasted_iota(jnp.int32, (flen, blocks * LANES), 1)
    lane_group = lax.rem(lane_group, LANES) // width
    factor = HD ** (-0.5) * math.log2(math.e)

    def fold(values, op):
        result = values[:, :LANES]
        for c in range(1, values.shape[1] // LANES):
            result = op(result, values[:, c * LANES : (c + 1) * LANES])
        return result

    def filter_block(i):
        @pl.loop(0, 3)
        def _(s):
            for h in range(heads):
                lanes = pl.ds(h * LANES, LANES)
                window = [
                    buf[s, pl.ds(pl.multiple_of(i * rows + b * flen, flen), 2 * flen), lanes]
                    for b in range(blocks)
                ]
                matrix = toep[s, pl.ds(h * per_tile * flen, per_tile * flen), :]
                product = jnp.dot(
                    matrix, jnp.concatenate(window, axis=1), preferred_element_type=jnp.float32
                )
                result = product[:flen]
                for g in range(1, per_tile):
                    result = jnp.where(
                        lane_group == g, product[g * flen : (g + 1) * flen], result
                    )
                result = result.astype(feat.dtype)
                for b in range(blocks):
                    feat[
                        s, pl.ds(pl.multiple_of(i * rows + b * flen, flen), flen), lanes
                    ] = result[:, b * LANES : (b + 1) * LANES]

    def rows_at(j):
        return pl.ds(pl.multiple_of(j * rows, flen), rows)

    def score(q, key, h):
        lanes = pl.ds(h * HD, HD)
        return lax.dot_general(
            feat[0, rows_at(q), lanes],
            feat[1, rows_at(key), lanes],
            (((1,), (1,)), ((), ())),
            preferred_element_type=jnp.float32,
        )

    def mixed(weights, key, h):
        return jnp.dot(
            weights.astype(jnp.bfloat16),
            feat[2, rows_at(key), pl.ds(h * HD, HD)],
            preferred_element_type=jnp.float32,
        )

    def open_block(q, h):
        place = lax.broadcasted_iota(jnp.int32, (rows, rows), 0)
        other = lax.broadcasted_iota(jnp.int32, (rows, rows), 1)
        block = jnp.where(other <= place, score(q, q, h), -1e30)
        new = jnp.max(fold(block, jnp.maximum), axis=1, keepdims=True)
        weights = jnp.exp2((block - new) * factor)
        at = q * heads + h
        top[at] = jnp.broadcast_to(new, (rows, LANES))
        total[at] = fold(weights, jnp.add)
        accum[at] = mixed(weights, q, h)

    def add_block(q, key, h):
        at = q * heads + h
        block = score(q, key, h)
        old = top[at]
        new = jnp.maximum(old, jnp.max(fold(block, jnp.maximum), axis=1, keepdims=True))
        shrink = jnp.exp2((old - new) * factor)
        weights = jnp.exp2((block - new[:, :1]) * factor)
        top[at] = new
        total[at] = total[at] * shrink + fold(weights, jnp.add)
        accum[at] = accum[at] * shrink + mixed(weights, key, h)

    def close_block(q, h):
        at = q * heads + h
        sum_of = jnp.sum(total[at], axis=1, keepdims=True)
        return (accum[at] / sum_of).astype(jnp.bfloat16)

    def back_copy(target, source):
        return pltpu.make_async_remote_copy(
            src_ref=sending.at[target],
            dst_ref=att.at[:, col_of(source)],
            send_sem=back_send.at[target],
            recv_sem=back_recv.at[source],
            device_id={"ctx": target},
            device_id_type=MESH,
        )

    for k in range(1, n):
        source = source_at(k)
        stream_copy(0, source, source).wait_recv()
    own_copy().wait()

    @pl.loop(0, n)
    def _(k):
        b = source_at(k)

        @pl.when(k > 0)
        def _():
            stream_copy(1, b, b).wait_recv()

        filter_block(b)
        for h in range(heads):
            open_block(b, h)

            @pl.loop(0, k)
            def _(before):
                o = source_at(before)
                add_block(jnp.maximum(b, o), jnp.minimum(b, o), h)

    @pl.loop(0, n)
    def _(k):
        i = source_at(n - 1 - k)
        for h in range(heads):
            sending[i, :, pl.ds(h * HD, HD)] = close_block(i, h)

        @pl.when(i != me)
        def _():
            back_copy(i, me).start()

        @pl.when(i == me)
        def _():
            att[:, col_of(me)] = sending[i]

    for k in range(1, n):
        source = lax.rem(me + k, n)
        back_copy(source, source).wait_recv()

    @pl.loop(0, blocks)
    def _(b):
        part = pl.ds(pl.multiple_of(b * flen, flen), flen)
        wide = att[part, :].astype(jnp.float32)
        squares = fold(wide * wide, jnp.add).T
        squares = squares.reshape(LANES // 8, 8, flen)
        sums[0, :, part] = jnp.sum(squares, axis=0)

    def sum_copy(k, turn):
        return pltpu.make_async_remote_copy(
            src_ref=sums.at[0],
            dst_ref=sums.at[k],
            send_sem=sum_send.at[k],
            recv_sem=sum_recv.at[k],
            device_id={"grp": lax.rem(my_grp + turn, n_grp)},
            device_id_type=MESH,
        )

    for k in range(1, n_grp):
        sum_copy(k, k).start()
    for k in range(1, n_grp):
        sum_copy(k, k).wait()

    @pl.loop(0, blocks)
    def _(b):
        part = pl.ds(pl.multiple_of(b * flen, flen), flen)
        power = sums[0, :, part]
        for k in range(1, n_grp):
            power = power + sums[k, :, part]
        power = jnp.sum(power, axis=0, keepdims=True) / (chans * n_grp)
        power = jnp.broadcast_to(lax.rsqrt(power + 1e-06), (LANES, flen)).T
        wide = att[part, :].astype(jnp.float32)
        for c in range(chans // LANES):
            lanes = slice(c * LANES, (c + 1) * LANES)
            out[part, lanes] = (wide[:, lanes] * gain[:, lanes] * power).astype(out.dtype)

    for k in range(1, n):
        target = lax.rem(me + k, n)
        for p in range(2):
            stream_copy(p, target, me).wait_send()
        back_copy(target, me).wait_send()


def fused(streams, filters, gain):
    n, n_grp = lax.axis_size("ctx"), lax.axis_size("grp")
    _, rows, chans = streams.shape
    _, groups, flen = filters.shape
    cols = chans // n
    tokens = rows * n
    vmem = pl.BlockSpec(memory_space=pltpu.VMEM)
    return pl.pallas_call(
        functools.partial(fused_kernel, n, n_grp),
        out_shape=jax.ShapeDtypeStruct((rows, chans), jnp.bfloat16),
        in_specs=[pl.BlockSpec(memory_space=pl.ANY), vmem, vmem],
        out_specs=vmem,
        scratch_shapes=[
            pltpu.VMEM((3, flen + tokens, cols), jnp.bfloat16),
            pltpu.VMEM((3, groups, flen), jnp.float32),
            pltpu.VMEM((3, groups // n * flen, 2 * flen), jnp.bfloat16),
            pltpu.VMEM((3, tokens, cols), jnp.bfloat16),
            pltpu.VMEM((chans // HD, rows, LANES), jnp.float32),
            pltpu.VMEM((chans // HD, rows, LANES), jnp.float32),
            pltpu.VMEM((chans // HD, rows, HD), jnp.float32),
            pltpu.VMEM((n, rows, cols), jnp.bfloat16),
            pltpu.VMEM((rows, chans), jnp.bfloat16),
            pltpu.VMEM((n_grp, 8, rows), jnp.float32),
            pltpu.SemaphoreType.DMA((1,)),
            pltpu.SemaphoreType.DMA((n, 2)),
            pltpu.SemaphoreType.DMA((n, 2)),
            pltpu.SemaphoreType.DMA((n,)),
            pltpu.SemaphoreType.DMA((n,)),
            pltpu.SemaphoreType.DMA((n_grp,)),
            pltpu.SemaphoreType.DMA((n_grp,)),
        ],
        compiler_params=pltpu.CompilerParams(collective_id=0, has_side_effects=True),
        name="fused",
    )(streams, filters, gain.reshape(1, chans))


def passed_along(block, axis, distance):
    devices = range(lax.axis_size(axis))
    route = [(i - distance, i) for i in devices if i - distance in devices]
    return lax.ppermute(block, axis, route)


def filter_all(streams, filters):
    tok_rows = streams.shape[1]
    chan_count = streams.shape[2]
    filt_len = filters.shape[2]
    group_count = filters.shape[1]
    group_width = chan_count // group_count
    tail = streams[:, tok_rows - filt_len :, :]
    before = passed_along(tail, "ctx", 1)
    padded = jnp.concatenate([before, streams], axis=1)
    block_count = tok_rows // filt_len
    blocks = padded.reshape(3, block_count + 1, filt_len, group_count, group_width)
    lag_table = np.arange(filt_len)[:, None] - np.arange(filt_len)[None, :]
    lower_idx = np.where(lag_table >= 0, lag_table, 0)
    upper_idx = np.where(lag_table < 0, lag_table + filt_len, 0)
    lower = jnp.where(lag_table >= 0, filters[:, :, lower_idx], 0.0)
    upper = jnp.where(lag_table < 0, filters[:, :, upper_idx], 0.0)
    result = jnp.einsum(
        "agts,absgc->abtgc", lower, blocks[:, 1:], preferred_element_type=jnp.float32
    )
    result = result + jnp.einsum(
        "agts,absgc->abtgc", upper, blocks[:, :-1], preferred_element_type=jnp.float32
    )
    return result.reshape(3, tok_rows, chan_count).astype(jnp.bfloat16)


def attend(queries, positions, keyed, valued):
    tok_rows, chan_count = queries.shape
    head_count = chan_count // HD
    scale = HD ** (-0.5)
    query_heads = queries.reshape(tok_rows, head_count, HD)
    query_last = jnp.max(positions)
    start_state = (
        jnp.full((head_count, tok_rows), -1e30, jnp.float32),
        jnp.zeros((head_count, tok_rows), jnp.float32),
        jnp.zeros((tok_rows, head_count, HD), jnp.float32),
    )
    key_piece = lax.all_gather(keyed, "ctx", axis=0, tiled=True)
    value_piece = lax.all_gather(valued, "ctx", axis=0, tiled=True)
    piece_len = key_piece.shape[0]
    block_len = math.gcd(piece_len, 512)

    def step_block(step_idx, state):
        offset = step_idx * block_len
        key_block = lax.dynamic_slice_in_dim(key_piece, offset, block_len, 0).reshape(
            block_len, head_count, HD
        )
        value_block = lax.dynamic_slice_in_dim(value_piece, offset, block_len, 0).reshape(
            block_len, head_count, HD
        )
        key_pos = offset + jnp.arange(block_len, dtype=jnp.int32)

        def update_block(inner):
            running, totals, accum = inner
            scores = (
                jnp.einsum(
                    "shd,khd->hsk", query_heads, key_block, preferred_element_type=jnp.float32
                )
                * scale
            )
            causal = key_pos[None, None, :] <= positions[None, :, None]
            newtop = jnp.maximum(running, jnp.max(jnp.where(causal, scores, -1e30), axis=2))
            weights = jnp.where(causal, jnp.exp(scores - newtop[:, :, None]), 0.0)
            factor = jnp.exp(running - newtop)
            totals = totals * factor + jnp.sum(weights, axis=2)
            accum = accum * factor.T[:, :, None] + jnp.einsum(
                "hsk,khd->shd",
                weights.astype(jnp.bfloat16),
                value_block,
                preferred_element_type=jnp.float32,
            )
            return (newtop, totals, accum)

        return lax.cond(offset > query_last, lambda inner: inner, update_block, state)

    running, totals, accum = lax.fori_loop(0, piece_len // block_len, step_block, start_state)
    return (accum / totals.T[:, :, None]).reshape(tok_rows, chan_count).astype(jnp.bfloat16)


def local(streams, filters, gain):
    features = filter_all(streams, filters)
    tok_rows = streams.shape[1]
    my_index = lax.axis_index("ctx")
    queries = features[0]
    positions = my_index * tok_rows + jnp.arange(tok_rows, dtype=jnp.int32)
    attended = attend(queries, positions, features[1], features[2])
    wide = attended.astype(jnp.float32)
    power = lax.psum(jnp.sum(wide * wide, axis=1), "grp") / (streams.shape[2] * lax.axis_size("grp"))
    return (wide * gain[None, :] * lax.rsqrt(power + 1e-06)[:, None]).astype(jnp.bfloat16)


def chosen(streams, filters, gain):
    n = lax.axis_size("ctx")
    _, rows, chans = streams.shape
    _, groups, flen = filters.shape
    whole_heads = chans % (n * HD) == 0
    fits = flen == LANES and rows % flen == 0 and LANES % (chans // groups) == 0
    if n > 1 and whole_heads and fits and groups % n == 0:
        return fused(streams, filters, gain)
    return local(streams, filters, gain)


def solution(mesh):
    placed = (P(None, "ctx", "grp"), P(None, "grp", None), P("grp"))
    return jax.shard_map(
        chosen, mesh=mesh, in_specs=placed, out_specs=P("ctx", "grp"), check_vma=False
    )
```
